512 devices in a mesh: cp: 64 (over y, x, z_lo), sp: 8 (over z_hi, core).
Axes of the slice: x: 4, y: 4, z: 16 (z_hi: 4, z_lo: 4; z = z_hi * 4 + z_lo), core: 2. Of those that a mesh axis runs over, the one named last changes fastest.
Arguments:
- queries: bfloat16 [16384, 2048], P('cp', 'sp'), may hold values from -22 to 22
- keys: bfloat16 [16384, 128], P(('cp', 'sp')), may hold values from -5 to 5
- values: bfloat16 [16384, 128], P(('cp', 'sp')), may hold values from -6 to 6
- doc_ids: int32 [128], replicated, may hold values from 0 to 31, never falling along the last dimension, each value on 1 to 32 neighbouring positions
- span_order: int32 [64], replicated, may hold values from 0 to 63, each once
Outputs:
- attended: bfloat16 [16384, 2048], P('cp', 'sp')
The draws below stay inside these ranges and needn't reach their ends.
Inputs may be any that keep to these rules, and one draw needn't show every extreme that they name: doc_ids never falls; each document covers 1 to 32 consecutive blocks, and one covers exactly 32. Index i of cp holds span span_order[i] of the sequence; each span once.
All inputs are finite; a program needn't handle non-finite values.
Results may differ from the reference program's by a relative error of at most 0.0036.
Values may be sent and summed in bfloat16 or wider, within the bound.
A program may use at most 64 MiB of HBM per device.

```python
import math
import jax
import jax.numpy as jnp
import numpy as np
from jax import lax

HD = 128
HEADS = 16
SPAN = 256
BLK = 128
SEQ = 16384
NBLK = 128
MOST = 32
N_CP = 64


def paired_draw(key):
    key_rows = jnp.clip(jax.random.normal(jax.random.fold_in(key, 11), (SEQ, HD), jnp.float32), -5.0, 5.0)
    query_rows = jnp.clip(jax.random.normal(jax.random.fold_in(key, 14), (SEQ, HEADS, HD), jnp.float32), -5.0, 5.0)
    return (query_rows.reshape(SEQ, HEADS * HD), key_rows)


def draw_queries(key, part):
    query_rows, key_rows = paired_draw(key)
    return query_rows.astype(jnp.bfloat16)


def draw_keys(key, part):
    query_rows, key_rows = paired_draw(key)
    return key_rows.astype(jnp.bfloat16)


def level_of(rng, dims, shards, smallest, top_value):
    loudness = 1.0
    for axis_at, blocks in shards:
        steps = jax.random.uniform(jax.random.fold_in(jax.random.fold_in(rng, 6), axis_at), (blocks,), jnp.float32, smallest / len(shards), top_value / len(shards))
        loudness = loudness * jnp.repeat(jnp.exp(steps), dims[axis_at] // blocks).reshape((-1,) + (1,) * (len(dims) - 1 - axis_at))
    return loudness


def profile(number_of, total, most, skew):
    portions = [(1 << 20) // math.isqrt(standing ** skew) + 1 for standing in range(2, number_of + 1)]
    surplus, holding = total - most - (number_of - 1), [1] * (number_of - 1)
    while surplus > 0:
        movable = [i for i in range(number_of - 1) if holding[i] < most]
        pool, remaining = sum([portions[i] for i in movable]), surplus
        for i in movable:
            addition = min(most - holding[i], max(1, remaining * portions[i] // pool), surplus)
            holding[i] = holding[i] + addition
            surplus = surplus - addition
    return np.array([most] + holding)


def uneven_parts(own_key, amount, total, most, lean):
    if amount == 2:
        one = jax.random.randint(own_key, (), max(1, total - most), min(most, total - 1) + 1)
        return jnp.stack([one, total - one])
    tallies = jnp.asarray(profile(amount, total, most, lean), jnp.int32)
    couples = (amount - 1) // 2
    source_of, receiver = tallies[1:1 + 2 * couples:2], tallies[2:2 + 2 * couples:2]
    margin = jnp.minimum(source_of - 1, most - receiver)
    moved = jax.random.randint(jax.random.fold_in(own_key, 1), (couples,), 0, 1 << 20) % (margin + 1)
    tallies = tallies.at[1:1 + 2 * couples:2].set(source_of - moved).at[2:2 + 2 * couples:2].set(receiver + moved)
    return tallies[jax.random.permutation(jax.random.fold_in(own_key, 2), amount)]


def bell_draw(rng, shape, spread, most, cuts=(), kind=jnp.bfloat16):
    gain = level_of(rng, shape, cuts, -0.22, 0.18) if cuts else 1.0
    values = jax.random.normal(rng, shape, jnp.float32) * spread * gain
    return jnp.minimum(jnp.maximum(values, -most), most).astype(kind)


def setup_inputs(seed: int = 0) -> dict:
    streams_of = jax.random.split(jax.random.key(seed), 6)
    return {
        "queries": draw_queries(jax.random.fold_in(streams_of[5], 71), 0),
        "keys": draw_keys(jax.random.fold_in(streams_of[5], 71), 0),
        "values": bell_draw(streams_of[2], (SEQ, HD), 1.0, 6.0, ((0, 512),)),
        "doc_ids": jnp.searchsorted(jnp.cumsum(uneven_parts(streams_of[3], NBLK // 4, NBLK, MOST, 2)), jnp.arange(NBLK), side="right").astype(jnp.int32),
        "span_order": jax.random.permutation(streams_of[4], N_CP).astype(jnp.int32),
    }


NEGATIVE = -1e+30

def reference(queries, keys, values, doc_ids, span_order):
    score_scale = 1.0 / math.sqrt(HD)

    def to_true(array):
        span_parts = array.reshape((N_CP, SPAN) + array.shape[1:])
        placed = jnp.zeros_like(span_parts).at[span_order].set(span_parts)
        return placed.reshape(array.shape)
    query_true = to_true(queries).reshape(SEQ, HEADS, HD)
    key_true = to_true(keys)
    value_true = to_true(values)
    front_pad = (MOST - 1) * BLK
    window = MOST * BLK
    key_padded = jnp.concatenate([jnp.zeros((front_pad, HD), keys.dtype), key_true], axis=0)
    value_padded = jnp.concatenate([jnp.zeros((front_pad, HD), values.dtype), value_true], axis=0)
    token_doc = jnp.repeat(doc_ids.astype(jnp.int32), BLK)
    doc_padded = jnp.concatenate([jnp.full((front_pad,), -1, jnp.int32), token_doc])

    def attend_block(block_index):
        first = (block_index * BLK).astype(jnp.int32)
        block_query = lax.dynamic_slice_in_dim(query_true, first, BLK, 0).astype(jnp.float32)
        block_key = lax.dynamic_slice_in_dim(key_padded, first, window, 0).astype(jnp.float32)
        block_value = lax.dynamic_slice_in_dim(value_padded, first, window, 0).astype(jnp.float32)
        query_doc = lax.dynamic_slice_in_dim(token_doc, first, BLK, 0)
        key_doc = lax.dynamic_slice_in_dim(doc_padded, first, window, 0)
        query_pos = first + jnp.arange(BLK, dtype=jnp.int32)
        key_pos = first - front_pad + jnp.arange(window, dtype=jnp.int32)
        allowed = (key_pos[None, :] <= query_pos[:, None]) & (key_doc[None, :] == query_doc[:, None])
        scores = jnp.einsum('qhd,kd->hqk', block_query, block_key, precision=lax.Precision.HIGHEST) * score_scale
        masked = jnp.where(allowed[None], scores, NEGATIVE)
        row_max = lax.optimization_barrier(jnp.max(masked, axis=2, keepdims=True))
        raw = jnp.where(allowed[None], jnp.exp(masked - row_max), 0.0)
        row_total = lax.optimization_barrier(jnp.sum(raw, axis=2))
        weights = lax.optimization_barrier(raw.astype(jnp.bfloat16)).astype(jnp.float32)
        numer = jnp.einsum('hqk,kd->qhd', weights, block_value, precision=lax.Precision.HIGHEST)
        return (numer / jnp.transpose(row_total)[:, :, None]).astype(jnp.bfloat16)
    blocks = lax.map(attend_block, jnp.arange(NBLK, dtype=jnp.int32))
    result_true = blocks.reshape(N_CP, SPAN, HEADS * HD)
    return result_true[span_order].reshape(SEQ, HEADS * HD)
```

```python
import functools
import math

import jax
import jax.numpy as jnp
from jax import lax
from jax.experimental import pallas as pl
from jax.experimental.pallas import tpu as pltpu
from jax.sharding import PartitionSpec as P

HD = 128
SPAN = 256
BLK = 128
MOST = 32
REACH = MOST * BLK // SPAN + 1
NEGATIVE = -1e30


def plan(doc_ids, span_order, cp_index):
    stored = jnp.arange(span_order.shape[0], dtype=jnp.int32)
    mine = jnp.sum(jnp.where(stored == cp_index, span_order, 0))
    blocks = jnp.arange(doc_ids.shape[0], dtype=jnp.int32)
    doc_first = jnp.sum(jnp.where(blocks == 2 * mine, doc_ids, 0))
    doc_second = jnp.sum(jnp.where(blocks == 2 * mine + 1, doc_ids, 0))
    low_first = jnp.sum((doc_ids < doc_first).astype(jnp.int32)) * BLK
    low_second = jnp.sum((doc_ids < doc_second).astype(jnp.int32)) * BLK
    count = mine - low_first // SPAN + 1
    wanted = mine - jnp.arange(REACH, dtype=jnp.int32)
    places = jnp.sum(jnp.where(span_order[None, :] == wanted[:, None], stored[None, :], 0), axis=1)
    head = jnp.stack([count, mine * SPAN, low_first, low_second])
    return jnp.concatenate([head, places]).astype(jnp.int32)


def group_rows(x, fold):
    return fold(x.reshape(x.shape[0] // 8, 8, x.shape[1]), axis=0)


def attend_kernel(plan_ref, query_ref, kv_ref, out_ref, held, scores, accum, sems):
    count, first_pos = plan_ref[0], plan_ref[1]
    low_first, low_second = plan_ref[2], plan_ref[3]
    rate = math.log2(math.e) / math.sqrt(HD)

    def copy_of(step):
        rows = pl.ds(pl.multiple_of(plan_ref[4 + step] * SPAN, SPAN), SPAN)
        return pltpu.make_async_copy(kv_ref.at[rows, :], held.at[step], sems.at[step])

    def start(step, carried):
        copy_of(step).start()
        return carried

    lax.fori_loop(0, count, start, 0)
    heads = query_ref.shape[1] // HD
    query = jnp.concatenate([query_ref[:, h * HD : (h + 1) * HD] for h in range(heads)], axis=0)
    width = query.shape[0]
    column = lax.broadcasted_iota(jnp.int32, (1, width), 1) % SPAN
    low = jnp.where(column < BLK, low_first, low_second)
    key_row = lax.broadcasted_iota(jnp.int32, (SPAN, width), 0)

    def score(step):
        copy_of(step).wait()
        return lax.dot_general(
            held[step, :, :HD], query, (((1,), (1,)), ((), ())), preferred_element_type=jnp.float32
        )

    first = score(0)
    first = jnp.where((key_row <= column) & (key_row >= low - first_pos), first, NEGATIVE)
    scores[0] = first

    def score_step(step, top):
        block = score(step)
        block = jnp.where(key_row >= low - (first_pos - step * SPAN), block, NEGATIVE)
        scores[step] = block
        return jnp.maximum(top, group_rows(block, jnp.max))

    top = lax.fori_loop(1, count, score_step, group_rows(first, jnp.max))
    top = jnp.max(top, axis=0, keepdims=True)
    accum[...] = jnp.zeros_like(accum)

    def value_step(step, total):
        weights = jnp.exp2((scores[step] - top) * rate)
        accum[...] += lax.dot_general(
            held[step, :, HD:],
            weights.astype(jnp.bfloat16),
            (((0,), (0,)), ((), ())),
            preferred_element_type=jnp.float32,
        )
        return total + group_rows(weights, jnp.sum)

    total = lax.fori_loop(0, count, value_step, jnp.zeros((8, width), jnp.float32))
    result = accum[...] / jnp.sum(total, axis=0, keepdims=True)
    for h in range(heads):
        piece = result[:, h * SPAN : (h + 1) * SPAN].T
        out_ref[:, h * HD : (h + 1) * HD] = piece.astype(out_ref.dtype)


def attend(where, queries, kv):
    width = queries.shape[0] * (queries.shape[1] // HD)
    return pl.pallas_call(
        attend_kernel,
        out_shape=jax.ShapeDtypeStruct(queries.shape, jnp.bfloat16),
        in_specs=[
            pl.BlockSpec(memory_space=pltpu.SMEM),
            pl.BlockSpec(memory_space=pltpu.VMEM),
            pl.BlockSpec(memory_space=pl.ANY),
        ],
        out_specs=pl.BlockSpec(memory_space=pltpu.VMEM),
        scratch_shapes=[
            pltpu.VMEM((REACH, SPAN, 2 * HD), jnp.bfloat16),
            pltpu.VMEM((REACH, SPAN, width), jnp.float32),
            pltpu.VMEM((HD, width), jnp.float32),
            pltpu.SemaphoreType.DMA((REACH,)),
        ],
        compiler_params=pltpu.CompilerParams(vmem_limit_bytes=48 << 20),
    )(where, queries, kv)


def shards(queries, keys, values, doc_ids, span_order):
    where = plan(doc_ids, span_order, lax.axis_index("cp"))
    kv = jnp.concatenate([keys, values], axis=1)
    kv = lax.all_gather(kv, ("cp", "sp"), axis=0, tiled=True)
    return attend(where, queries, kv)


def solution(mesh):
    in_specs = (P("cp", "sp"), P(("cp", "sp"), None), P(("cp", "sp"), None), P(), P())
    out_specs = P("cp", "sp")
    return jax.shard_map(shards, mesh=mesh, in_specs=in_specs, out_specs=out_specs, check_vma=False)
```
